32 devices in a mesh: groups: 2 (over x), ctx: 16 (over z, y, core).
Axes of the slice: x: 2, y: 2, z: 4, core: 2. Of those that a mesh axis runs over, the one named last changes fastest.
Arguments:
- queries: bfloat16 [4096, 1024], P(('groups', 'ctx')), parts along dimension 0, may hold values from -100 to 100
- encoder_rows: bfloat16 [3072, 2048], P(('groups', 'ctx')), parts along dimension 0, may hold values from -6 to 6
- key_weight: bfloat16 [2048, 1024], replicated, may hold values from -0.125 to 0.125
- value_weight: bfloat16 [2048, 1024], replicated, may hold values from -0.125 to 0.125
- out_weight: bfloat16 [1024, 2048], P(None, 'ctx'), may hold values from -0.1875 to 0.1875
Outputs:
- attended: bfloat16 [4096, 2048], P(('groups', 'ctx')), parts along dimension 0
The draws below stay inside these ranges and needn't reach their ends.
There are 2 independent parts, one for each index of `groups`. The reference program is written for one: setup_inputs(seed, part) draws one part's arguments, and reference() takes and returns one part's arrays. A program takes and returns all parts, laid end to end along the dimension named above; an argument that names none is the same for every part. Nothing has to cross between parts.
All inputs are finite; a program needn't handle non-finite values.
Results may differ from the reference program's by a relative error of at most 0.009.
The reference program's roundings to bfloat16 on the way (of `keys`, `values`, `weights` and `context`) count: a program that leaves them out, or rounds other values in their place, can miss the bound.
Values may be sent and summed in bfloat16 or wider, within the bound.
A program may use at most 192 MiB of HBM per device.

```python
import math
import jax
import jax.numpy as jnp
from jax import lax

D = 2048
HEADS = 16
DH = 64
HD = 1024
QTOK = 2048
ENC = 1536


def draw_queries(key, part):
    base = jax.random.normal(key, (QTOK, HEADS * DH), jnp.float32)
    vals = jnp.clip(base, -6.0, 6.0)
    return vals.astype(jnp.bfloat16)


def shard_levels(rng, dims, pieces, smallest, high):
    level = 1.0
    for axis_at, parts in pieces:
        draws = jax.random.uniform(jax.random.fold_in(jax.random.fold_in(rng, 6), axis_at), (parts,), jnp.float32, smallest / len(pieces), high / len(pieces))
        level = level * jnp.repeat(jnp.exp(draws), dims[axis_at] // parts).reshape((-1,) + (1,) * (len(dims) - 1 - axis_at))
    return level


def normal_values(stream_key, dims, deviation, reach, shards=(), dtype=jnp.bfloat16):
    array = deviation * jax.random.normal(stream_key, dims, jnp.float32)
    if shards:
        array = array * shard_levels(stream_key, dims, shards, -0.22, 0.18)
    return jnp.clip(array, -reach, reach).astype(dtype)


def setup_inputs(seed: int = 0, part: int = 0) -> dict:
    key_of = jax.random.split(jax.random.key(seed), 6)
    part_splits = jax.random.split(jax.random.fold_in(key_of[5], part), 6)
    return {
        "queries": draw_queries(jax.random.fold_in(jax.random.fold_in(key_of[5], part), 71), part),
        "encoder_rows": normal_values(part_splits[1], (ENC, D), 1.0, 6.0, ((0, 16),)),
        "key_weight": normal_values(key_of[2], (D, HD), D ** -0.5, 0.125),
        "value_weight": normal_values(key_of[3], (D, HD), D ** -0.5, 0.125),
        "out_weight": normal_values(key_of[4], (HD, D), HD ** -0.5, 0.1875, ((1, 16),)),
    }


def reference(queries, encoder_rows, key_weight, value_weight, out_weight):
    keys = jnp.dot(encoder_rows, key_weight, preferred_element_type=jnp.float32).astype(jnp.bfloat16)
    values = jnp.dot(encoder_rows, value_weight, preferred_element_type=jnp.float32).astype(jnp.bfloat16)
    keys3 = keys.reshape(ENC, HEADS, DH).astype(jnp.float32)
    values3 = values.reshape(ENC, HEADS, DH).astype(jnp.float32)
    block = math.gcd(QTOK, 512)
    blocks = queries.reshape(QTOK // block, block, HEADS, DH)

    def attend(query_block):
        scores = jnp.einsum("qhd,khd->hqk", query_block.astype(jnp.float32), keys3) * 0.125
        top = jnp.max(scores, axis=-1)
        expo = jnp.exp(scores - top[..., None])
        total = jnp.sum(expo, axis=-1)
        weights = expo.astype(jnp.bfloat16).astype(jnp.float32)
        summed = jnp.einsum("hqk,khd->qhd", weights, values3)
        context = (summed / jnp.transpose(total)[:, :, None]).astype(jnp.bfloat16).reshape(block, HD)
        return jnp.dot(context, out_weight, preferred_element_type=jnp.float32).astype(jnp.bfloat16)

    return lax.map(attend, blocks).reshape(QTOK, D)
```

```python
import functools
import math

import jax
import jax.numpy as jnp
from jax import lax
from jax.experimental import pallas as pl
from jax.experimental.pallas import tpu as pltpu
from jax.sharding import PartitionSpec as P

HEADS = 16
DH = 64
PAIR = 2 * DH
MESH = pl.DeviceIdType.MESH
LOG2E = 1.4426950408889634
FL = set()
EARLY = 8
UNROLL = 2
VLIM = 56


def kernel(
    groups, n, plane, chunks,
    q_hbm, e_hbm, kw_hbm, vw_hbm, ow_hbm, o_ref,
    q_ref, e_ref, kw, vw, qpack, kvpack, qall, kvall, keys2, vals2, cpack, call, ctx, wall,
    load_sem, own_sem, q_send, q_recv, kv_send, kv_recv, c_send, c_recv,
    z_send, z_recv, y_send, y_recv, x_send, x_recv, b_send, b_recv,
):
    grp = lax.axis_index("groups")
    me = lax.axis_index("ctx")
    rows = q_ref.shape[0]
    enc = e_ref.shape[0]
    depth = wall.shape[1]
    width = wall.shape[2]
    copies = n // HEADS
    share = rows // copies
    half = share // 2
    part = depth // groups
    layers = n // plane
    zed = me // plane
    spot = me % plane
    far = plane // 2
    over = zed * plane + (spot + far) % plane
    mate = zed * plane + (spot // 2) * 2 + (1 - spot % 2)
    heads = HEADS // chunks
    bf16 = jnp.bfloat16

    barrier = pltpu.get_barrier_semaphore()

    def greet(i, carry):
        pl.semaphore_signal(
            barrier, inc=1, device_id=(grp, (me + i) % n), device_id_type=MESH
        )
        return carry

    lax.fori_loop(1, n, greet, 0)
    for g in range(1, groups):
        pl.semaphore_signal(
            barrier, inc=1, device_id=((grp + g) % groups, me), device_id_type=MESH
        )

    load_q = pltpu.make_async_copy(q_hbm, q_ref, own_sem.at[0])
    load_w = pltpu.make_async_copy(ow_hbm, wall.at[me], own_sem.at[1])
    load_e = pltpu.make_async_copy(e_hbm, e_ref, own_sem.at[2])
    load_q.start()
    load_w.start()
    load_e.start()
    offsets = sorted(range(chunks), key=lambda i: (-min(i, chunks - i), i))

    def chunk_at(i):
        return (zed + offsets[i]) % chunks

    def loads(i):
        wide = kw.shape[2]
        cols = pl.ds(pl.multiple_of(chunk_at(i) * wide, wide), wide)
        return (
            pltpu.make_async_copy(kw_hbm.at[:, cols], kw.at[i], load_sem.at[i]),
            pltpu.make_async_copy(vw_hbm.at[:, cols], vw.at[i], load_sem.at[chunks + i]),
        )

    for i in range(chunks):
        for copy in loads(i):
            copy.start()

    def remote(src, dst, send, recv, to):
        return pltpu.make_async_remote_copy(
            src_ref=src, dst_ref=dst, send_sem=send, recv_sem=recv,
            device_id=to, device_id_type=MESH,
        )

    def q_copy(d, s):
        return remote(qpack.at[d], qall.at[s], q_send.at[d], q_recv.at[s], (grp, d))

    def kv_copy(d, s):
        return remote(
            kvpack.at[d % HEADS], kvall.at[pl.ds(s * enc, enc)],
            kv_send.at[d], kv_recv.at[s], (grp, d),
        )

    def c_copy(d, s):
        return remote(cpack.at[d], call.at[s], c_send.at[d], c_recv.at[s], (grp, d))

    mine = pl.ds(grp * part, part)

    def z_copy(src, way):
        block = wall.at[src * plane + spot, mine]
        to = zed + 1 - 2 * way
        return remote(
            block, block, z_send.at[way * layers + src], z_recv.at[src],
            (grp, to * plane + spot),
        )

    def hop(src, way, act):
        @pl.when((zed > 0) if way else (zed + 1 < layers))
        def _():
            act(z_copy(src, way))

    def y_copy(layer, at, to):
        block = wall.at[layer * plane + at, mine]
        return remote(block, block, y_send.at[layer], y_recv.at[layer], (grp, to))

    def near_copy(at, to):
        block = wall.at[zed * plane + at]
        return remote(block, block, y_send.at[zed], y_recv.at[zed], (grp, to))

    def x_copy(layer, side, g, whose):
        at = layer * plane + (spot + side * far) % plane
        block = wall.at[at, pl.ds(whose * part, part)]
        slot = (g * 2 + side) * layers + layer
        return remote(
            block, block, x_send.at[slot], x_recv.at[slot], ((grp + g) % groups, me)
        )

    def b_copy(layer, side, g, at):
        whose = (grp + groups - g) % groups
        block = wall.at[layer * plane + (at + side * far) % plane, pl.ds(whose * part, part)]
        slot = (g * 2 + side) * layers + layer
        return remote(block, block, b_send.at[slot], b_recv.at[slot], (grp, mate))

    def whole_copy(side, at):
        block = wall.at[zed * plane + (at + side * far) % plane]
        slot = side * layers + zed
        return remote(block, block, b_send.at[slot], b_recv.at[slot], (grp, mate))

    def some(first, last, body):
        def step(i, carry):
            body((me + i) % n)
            return carry

        lax.fori_loop(first, last, step, 0)

    def others(body):
        some(1, n, body)

    def beyond(body):
        def step(i, carry):
            body((zed + i) % layers)
            return carry

        lax.fori_loop(1, layers, step, 0)

    def far_first(body):
        def step(i, carry):
            d = (me + n // 2 + i) % n

            @pl.when(d != me)
            def _():
                body(d)

            return carry

        lax.fori_loop(0, n, step, 0)

    def sources(k, body):
        for way in range(2):
            src = zed + k if way else zed - k

            @pl.when((src < layers) if way else (src >= 0))
            def _():
                body(src, way)

    def on_z(src, way):
        z_copy(src, way).wait_recv()
        hop(src, way, lambda copy: copy.start())
        y_copy(src, spot, over).start()
        for g in range(1, groups):
            x_copy(src, 0, g, grp).start()
        b_copy(src, 0, 0, spot).start()

    def on_y(src, way):
        y_copy(src, (spot + far) % plane, over).wait_recv()
        for g in range(1, groups):
            x_copy(src, 1, g, grp).start()
        b_copy(src, 1, 0, spot).start()

    def on_x(src, way):
        for g in range(1, groups):
            for side in range(2):
                x_copy(src, side, g, (grp + groups - g) % groups).wait_recv()
                b_copy(src, side, g, spot).start()

    def on_near():
        near_copy((spot + far) % plane, over).wait_recv()
        whole_copy(1, spot).start()

    events = []
    for k in range(1, layers):
        events.append(functools.partial(sources, k, on_z))
        if k == 1:
            events.append(on_near)
        events.append(functools.partial(sources, k, on_y))
        if k > 1:
            events.append(functools.partial(sources, k - 1, on_x))
    events.append(functools.partial(sources, layers - 1, on_x))
    if 'now' in FL:
        events = []
    early = len(events) * EARLY // 16

    load_q.wait()
    for d in range(n):
        r0, c0 = (d // HEADS) * share, (d % HEADS) * DH
        qpack[d] = jnp.concatenate(
            [q_ref[r0 : r0 + half, c0 : c0 + DH], q_ref[r0 + half : r0 + share, c0 : c0 + DH]],
            axis=1,
        )
    load_w.wait()
    pl.semaphore_wait(barrier, n - 1 + groups - 1)
    if 'now' not in FL:
        hop(zed, 0, lambda copy: copy.start())
        hop(zed, 1, lambda copy: copy.start())
    far_first(lambda d: q_copy(d, me).start())
    if 'now' not in FL:
        near_copy(spot, over).start()
        whole_copy(0, spot).start()
    qall[me] = qpack[me]

    load_e.wait()
    for i in range(chunks):
        one, two = loads(i)
        one.wait()
        two.wait()
        j = chunk_at(i)
        keys = jnp.dot(e_ref[...], kw[i], preferred_element_type=jnp.float32).astype(bf16)
        values = jnp.dot(e_ref[...], vw[i], preferred_element_type=jnp.float32).astype(bf16)
        for h in range(heads):
            cols = slice(h * DH, (h + 1) * DH)
            kvpack[j * heads + h] = jnp.concatenate([keys[:, cols], values[:, cols]], axis=1)
        for c in range(copies):
            for h in range(heads):
                d = c * HEADS + j * heads + (h + spot) % heads

                @pl.when(d != me)
                def _(d=d):
                    kv_copy(d, me).start()

    kvall[pl.ds(me * enc, enc)] = kvpack[me % HEADS]
    for event in events[:early]:
        event()
    others(lambda s: q_copy(s, s).wait_recv())
    others(lambda s: kv_copy(s, s).wait_recv())

    memory = kvall[...]
    nothing, ones = jnp.zeros((n * enc, DH), bf16), jnp.ones((n * enc, DH), bf16)
    keys2[0] = jnp.concatenate([memory[:, :DH], nothing], axis=1)
    keys2[1] = jnp.concatenate([nothing, memory[:, :DH]], axis=1)
    vals2[0] = jnp.concatenate([memory[:, DH:], ones], axis=1)
    vals2[1] = jnp.concatenate([ones, memory[:, DH:]], axis=1)

    together = min(n, max(1, 256 // half))
    left = lax.broadcasted_iota(jnp.int32, (together * half, PAIR), 1) < DH

    def attend(i):
        whose = [(me + n // 2 + i * together + j) % n for j in range(together)]
        query = jnp.concatenate([qall[s] for s in whose], axis=0)
        summed = []
        for side in range(2):
            scores = lax.dot_general(
                query, keys2[side], (((1,), (1,)), ((), ())), preferred_element_type=jnp.float32
            )
            top = jnp.max(scores, axis=1, keepdims=True)
            expo = jnp.exp2((scores - top) * (0.125 * LOG2E)).astype(bf16)
            summed.append(jnp.dot(expo, vals2[side], preferred_element_type=jnp.float32))
        over_total = jnp.where(left, summed[1], summed[0])
        out = (jnp.where(left, summed[0], summed[1]) / pltpu.roll(over_total, DH, 1)).astype(bf16)
        for j, s in enumerate(whose):
            cpack[s] = out[j * half : (j + 1) * half]
        return whose

    def send(whose):
        for s in whose:

            @pl.when(s != me)
            def _(s=s):
                c_copy(s, me).start()

    steps = n // together
    unroll = math.gcd(steps, UNROLL)
    late = events[early:]
    turns = steps // unroll
    for t in range(turns):
        whose = []
        for u in range(unroll):
            whose += attend(t * unroll + u)
        send(whose)
        for event in late[len(late) * t // turns : len(late) * (t + 1) // turns]:
            event()

    call[me] = cpack[me]
    others(lambda s: c_copy(s, s).wait_recv())
    for c in range(copies):
        for j in range(HEADS // 2):
            one, two = call[c * HEADS + 2 * j], call[c * HEADS + 2 * j + 1]
            r0, cols = c * share, slice(j * PAIR, (j + 1) * PAIR)
            ctx[r0 : r0 + half, cols] = jnp.concatenate([one[:, :DH], two[:, :DH]], axis=1)
            ctx[r0 + half : r0 + share, cols] = jnp.concatenate([one[:, DH:], two[:, DH:]], axis=1)

    mates = mate % plane

    def take_b(z):
        for g in range(groups):
            for side in range(2):
                b_copy(z, side, g, mates).wait_recv()

    if 'now' not in FL:
        whole_copy(0, mates).wait_recv()
        whole_copy(1, mates).wait_recv()
        beyond(take_b)
    for d in range(0, n, 2):
        pair = jnp.concatenate([wall[d], wall[d + 1]], axis=1)
        o_ref[:, d * width : (d + 2) * width] = jnp.dot(
            ctx[...], pair, preferred_element_type=jnp.float32
        ).astype(bf16)

    def sent(d):
        q_copy(d, me).wait_send()
        kv_copy(d, me).wait_send()
        c_copy(d, me).wait_send()

    others(sent)
    if 'now' in FL:
        return

    def sent_layer(z):
        y_copy(z, spot, over).wait_send()
        for side in range(2):
            for g in range(1, groups):
                x_copy(z, side, g, grp).wait_send()
            for g in range(groups):
                b_copy(z, side, g, spot).wait_send()

    beyond(sent_layer)

    def sent_hop(z, carry):
        @pl.when(z <= zed)
        def _():
            hop(z, 0, lambda copy: copy.wait_send())

        @pl.when(z >= zed)
        def _():
            hop(z, 1, lambda copy: copy.wait_send())

        return carry

    lax.fori_loop(0, layers, sent_hop, 0)
    near_copy(spot, over).wait_send()
    whole_copy(0, spot).wait_send()
    whole_copy(1, spot).wait_send()


def per_device(groups, n, queries, encoder_rows, key_weight, value_weight, out_weight):
    rows, wide = queries.shape
    enc, model = encoder_rows.shape
    depth, width = out_weight.shape
    plane = math.gcd(n, 4)
    layers = n // plane
    chunks = 4
    half = rows // (n // HEADS) // 2
    bf16 = jnp.bfloat16
    dma = lambda k: pltpu.SemaphoreType.DMA((k,))
    hbm = pl.BlockSpec(memory_space=pl.ANY)
    return pl.pallas_call(
        functools.partial(kernel, groups, n, plane, chunks),
        out_shape=pltpu.VMEM((rows, n * width), bf16),
        in_specs=[hbm] * 5,
        out_specs=pl.BlockSpec(memory_space=pltpu.VMEM),
        scratch_shapes=[
            pltpu.VMEM((rows, wide), bf16),
            pltpu.VMEM((enc, model), bf16),
            pltpu.VMEM((chunks, model, wide // chunks), bf16),
            pltpu.VMEM((chunks, model, wide // chunks), bf16),
            pltpu.VMEM((n, half, PAIR), bf16),
            pltpu.VMEM((HEADS, enc, PAIR), bf16),
            pltpu.VMEM((n, half, PAIR), bf16),
            pltpu.VMEM((n * enc, PAIR), bf16),
            pltpu.VMEM((2, n * enc, PAIR), bf16),
            pltpu.VMEM((2, n * enc, PAIR), bf16),
            pltpu.VMEM((n, half, PAIR), bf16),
            pltpu.VMEM((n, half, PAIR), bf16),
            pltpu.VMEM((rows, depth), bf16),
            pltpu.VMEM((n, depth, width), bf16),
            dma(2 * chunks),
            dma(3),
            dma(n), dma(n), dma(n), dma(n), dma(n), dma(n),
            dma(2 * layers), dma(layers), dma(layers), dma(layers),
            dma(2 * groups * layers), dma(2 * groups * layers),
            dma(2 * groups * layers), dma(2 * groups * layers),
        ],
        compiler_params=pltpu.CompilerParams(
            collective_id=0, has_side_effects=True, vmem_limit_bytes=VLIM * 1024 * 1024
        ),
    )(queries, encoder_rows, key_weight, value_weight, out_weight)


def solution(mesh):
    groups, n = mesh.shape["groups"], mesh.shape["ctx"]
    return jax.shard_map(
        functools.partial(per_device, groups, n),
        mesh=mesh,
        in_specs=(P(("groups", "ctx"), None), P(("groups", "ctx"), None), P(), P(), P(None, "ctx")),
        out_specs=P(("groups", "ctx"), None),
        check_vma=False,
    )
```

```python
import functools
import math

import jax
import jax.numpy as jnp
from jax import lax
from jax.experimental import pallas as pl
from jax.experimental.pallas import tpu as pltpu
from jax.sharding import PartitionSpec as P

HEADS = 16
DH = 64
PAIR = 2 * DH
MESH = pl.DeviceIdType.MESH
LOG2E = 1.4426950408889634
ORDER = (
    "o", "n", "p0", "p1", "p2", "p3", "Q", "q0", "z1", "y0", "r1", "q2",
    "q1", "y1", "z2", "q3", "K", "r2", "a0", "x1", "x0", "y2", "a1", "z3",
    "a2", "a3", "y3", "x2", "x3",
)


def kernel(
    groups, n, plane, chunks,
    q_hbm, e_hbm, kw_hbm, vw_hbm, ow_hbm, o_ref,
    q_ref, e_ref, kw, vw, qpack, kvpack, qall, kvall, keys2, vals2, cpack, call, ctx, wall,
    load_sem, own_sem, q_send, q_recv, kv_send, kv_recv, c_send, c_recv,
    z_send, z_recv, y_send, y_recv, x_send, x_recv, b_send, b_recv,
):
    grp = lax.axis_index("groups")
    me = lax.axis_index("ctx")
    rows = q_ref.shape[0]
    enc = e_ref.shape[0]
    depth = wall.shape[1]
    width = wall.shape[2]
    copies = n // HEADS
    share = rows // copies
    half = share // 2
    part = depth // groups
    layers = n // plane
    zed = me // plane
    spot = me % plane
    far = plane // 2
    over = zed * plane + (spot + far) % plane
    mate = zed * plane + (spot // 2) * 2 + (1 - spot % 2)
    heads = HEADS // chunks
    bf16 = jnp.bfloat16

    barrier = pltpu.get_barrier_semaphore()

    def greet(i, carry):
        pl.semaphore_signal(
            barrier, inc=1, device_id=(grp, (me + i) % n), device_id_type=MESH
        )
        return carry

    lax.fori_loop(1, n, greet, 0)
    for g in range(1, groups):
        pl.semaphore_signal(
            barrier, inc=1, device_id=((grp + g) % groups, me), device_id_type=MESH
        )

    load_q = pltpu.make_async_copy(q_hbm, q_ref, own_sem.at[0])
    load_w = pltpu.make_async_copy(ow_hbm, wall.at[me], own_sem.at[1])
    load_e = pltpu.make_async_copy(e_hbm, e_ref, own_sem.at[2])
    offsets = sorted(range(chunks), key=lambda i: (-min(i, chunks - i), i))

    def chunk_at(i):
        return (zed + offsets[i]) % chunks

    def loads(i):
        wide = kw.shape[2]
        cols = pl.ds(pl.multiple_of(chunk_at(i) * wide, wide), wide)
        return (
            pltpu.make_async_copy(kw_hbm.at[:, cols], kw.at[i], load_sem.at[i]),
            pltpu.make_async_copy(vw_hbm.at[:, cols], vw.at[i], load_sem.at[chunks + i]),
        )

    load_e.start()
    for i in range(chunks):
        for copy in loads(i):
            copy.start()
        if i == 0:
            load_q.start()
            load_w.start()

    def remote(src, dst, send, recv, to):
        return pltpu.make_async_remote_copy(
            src_ref=src, dst_ref=dst, send_sem=send, recv_sem=recv,
            device_id=to, device_id_type=MESH,
        )

    def q_copy(d, s):
        return remote(qpack.at[d], qall.at[s], q_send.at[d], q_recv.at[s], (grp, d))

    def kv_copy(d, s):
        return remote(
            kvpack.at[d % HEADS], kvall.at[pl.ds(s * enc, enc)],
            kv_send.at[d], kv_recv.at[s], (grp, d),
        )

    def c_copy(d, s):
        return remote(cpack.at[d], call.at[s], c_send.at[d], c_recv.at[s], (grp, d))

    mine = pl.ds(grp * part, part)

    def z_copy(src, to, own=False):
        block = wall.at[src * plane + spot, mine]
        return remote(
            ow_hbm.at[mine] if own else block, block, z_send.at[src * layers + to], z_recv.at[src],
            (grp, to * plane + spot),
        )

    def hop(act, across):
        if across:
            return

        @pl.when(zed + 1 < layers)
        def _():
            act(z_copy(zed, zed + 1, True))

        @pl.when(zed > 0)
        def _():
            act(z_copy(zed, zed - 1, True))

    def relay(src, act):
        @pl.when((src < zed) & (zed + 1 < layers))
        def _():
            act(z_copy(src, zed + 1))

        @pl.when((src > zed) & (zed > 0))
        def _():
            act(z_copy(src, zed - 1))

    def y_copy(layer, at, to, own=False):
        block = wall.at[layer * plane + at, mine]
        return remote(ow_hbm.at[mine] if own else block, block, y_send.at[layer], y_recv.at[layer], (grp, to))

    def x_copy(layer, side, g, whose):
        at = layer * plane + (spot + side * far) % plane
        block = wall.at[at, pl.ds(whose * part, part)]
        slot = (g * 2 + side) * layers + layer
        return remote(
            block, block, x_send.at[slot], x_recv.at[slot], ((grp + g) % groups, me)
        )

    def b_copy(layer, side, g, at):
        whose = (grp + groups - g) % groups
        block = wall.at[layer * plane + (at + side * far) % plane, pl.ds(whose * part, part)]
        slot = (g * 2 + side) * layers + layer
        return remote(block, block, b_send.at[slot], b_recv.at[slot], (grp, mate))

    def whole_copy(side, at):
        block = wall.at[zed * plane + (at + side * far) % plane]
        slot = side * layers + zed
        return remote(ow_hbm, block, b_send.at[slot], b_recv.at[slot], (grp, mate))

    def some(first, last, body):
        def step(i, carry):
            body((me + i) % n)
            return carry

        lax.fori_loop(first, last, step, 0)

    def others(body):
        some(1, n, body)

    def beyond(body):
        def step(i, carry):
            body((zed + i) % layers)
            return carry

        lax.fori_loop(1, layers, step, 0)

    def far_first(body):
        def step(i, carry):
            d = (me + n // 2 + i) % n

            @pl.when(d != me)
            def _():
                body(d)

            return carry

        lax.fori_loop(0, n, step, 0)

    def sources(k, body):
        for src in (zed - k, zed + k):

            @pl.when((src >= 0) & (src < layers))
            def _(src=src):
                body(src)

    def on_z(src):
        z_copy(src, zed).wait_recv()
        y_copy(src, spot, over).start()
        for g in range(1, groups):
            x_copy(src, 0, g, grp).start()
        b_copy(src, 0, 0, spot).start()

    def on_y(src):
        y_copy(src, (spot + far) % plane, over).wait_recv()
        for g in range(1, groups):
            x_copy(src, 1, g, grp).start()
        b_copy(src, 1, 0, spot).start()

    def on_x(src):
        for g in range(1, groups):
            for side in range(2):
                x_copy(src, side, g, (grp + groups - g) % groups).wait_recv()
                b_copy(src, side, g, spot).start()

    def on_far(src):
        for g in range(1, groups):
            x_copy(src, 1, g, (grp + groups - g) % groups).wait_recv()
            b_copy(src, 1, g, spot).start()

    events = {"y0": lambda: on_y(zed), "x0": lambda: on_far(zed)}
    for k in range(1, layers):
        events[f"z{k}"] = functools.partial(sources, k, on_z)
        events[f"r{k}"] = functools.partial(sources, k, lambda src: relay(src, lambda copy: copy.start()))
        events[f"y{k}"] = functools.partial(sources, k, on_y)
        events[f"x{k}"] = functools.partial(sources, k, on_x)

    pl.semaphore_wait(barrier, n - 1 + groups - 1)
    def pack_q():
        load_q.wait()
        for d in range(n):
            r0, c0 = (d // HEADS) * share, (d % HEADS) * DH
            qpack[d] = jnp.concatenate(
                [q_ref[r0 : r0 + half, c0 : c0 + DH], q_ref[r0 + half : r0 + share, c0 : c0 + DH]],
                axis=1,
            )
        qall[me] = qpack[me]

    def start_own():
        hop(lambda copy: copy.start(), False)

    def start_across():
        hop(lambda copy: copy.start(), True)

    def start_near():
        y_copy(zed, spot, over, True).start()
        whole_copy(0, spot).start()

    def project(i):
        if i == 0:
            load_e.wait()
        one, two = loads(i)
        one.wait()
        two.wait()
        j = chunk_at(i)
        keys = jnp.dot(e_ref[...], kw[i], preferred_element_type=jnp.float32).astype(bf16)
        values = jnp.dot(e_ref[...], vw[i], preferred_element_type=jnp.float32).astype(bf16)
        for h in range(heads):
            cols = slice(h * DH, (h + 1) * DH)
            kvpack[j * heads + h] = jnp.concatenate([keys[:, cols], values[:, cols]], axis=1)

    def send_kv(i):
        j = chunk_at(i)
        for c in range(copies):
            for h in range(heads):
                d = c * HEADS + j * heads + (h + spot) % heads

                @pl.when(d != me)
                def _(d=d):
                    kv_copy(d, me).start()

    def project_and_send(i):
        project(i)
        send_kv(i)

    def apart(k):
        at, bit = me, 1
        while bit <= k:
            if k & bit:
                at = at + bit * (1 - 2 * (me // bit % 2))
            bit *= 2
        return at

    def send_q(first, last):
        for k in range(last - 1, first - 1, -1):
            if k:
                q_copy(apart(k), me).start()

    def take_kv():
        kvall[pl.ds(me * enc, enc)] = kvpack[me % HEADS]
        others(lambda s: kv_copy(s, s).wait_recv())
        memory = kvall[...]
        nothing, ones = jnp.zeros((n * enc, DH), bf16), jnp.ones((n * enc, DH), bf16)
        keys2[0] = jnp.concatenate([memory[:, :DH], nothing], axis=1)
        keys2[1] = jnp.concatenate([nothing, memory[:, :DH]], axis=1)
        vals2[0] = jnp.concatenate([memory[:, DH:], ones], axis=1)
        vals2[1] = jnp.concatenate([ones, memory[:, DH:]], axis=1)

    together = min(n, max(1, 256 // half))
    left = lax.broadcasted_iota(jnp.int32, (together * half, PAIR), 1) < DH

    steps = n // together

    def attend(i):
        whose = [apart(k) for k in range(i * together, (i + 1) * together)]
        for k, s in zip(range(i * together, (i + 1) * together), whose):
            if k:
                q_copy(s, s).wait_recv()

        query = jnp.concatenate([qall[s] for s in whose], axis=0)
        summed = []
        for side in range(2):
            scores = lax.dot_general(
                query, keys2[side], (((1,), (1,)), ((), ())), preferred_element_type=jnp.float32
            )
            top = jnp.max(scores, axis=1, keepdims=True)
            expo = jnp.exp2((scores - top) * (0.125 * LOG2E)).astype(bf16)
            summed.append(jnp.dot(expo, vals2[side], preferred_element_type=jnp.float32))
        over_total = jnp.where(left, summed[1], summed[0])
        out = (jnp.where(left, summed[0], summed[1]) / pltpu.roll(over_total, DH, 1)).astype(bf16)
        for j, s in enumerate(whose):
            cpack[s] = out[j * half : (j + 1) * half]
        return whose

    def send(whose):
        for s in whose:

            @pl.when(s != me)
            def _(s=s):
                c_copy(s, me).start()


    def turn(i):
        send(attend(i))

    steps = n // together
    acts = dict(events)
    acts["Q"] = pack_q
    acts["o"], acts["n"], acts["K"], acts["f"] = start_own, start_near, take_kv, start_across
    for i in range(chunks):
        acts[f"p{i}"] = functools.partial(project_and_send, i)
        acts[f"c{i}"] = functools.partial(project, i)
        acts[f"s{i}"] = functools.partial(send_kv, i)
    for i in range(4):
        acts[f"q{i}"] = functools.partial(send_q, n * i // 4, n * (i + 1) // 4)
    for i in range(steps):
        acts[f"a{i}"] = functools.partial(turn, i)
    rest = [f"a{i}" for i in range(steps)]
    for k in range(1, layers):
        rest += [f"z{k}", f"r{k}", f"y{k}", f"x{k}"]
    known = [name for name in ORDER if name in acts]
    for name in known + [name for name in rest if name not in known]:
        acts[name]()

    load_w.wait()
    call[me] = cpack[me]
    others(lambda s: c_copy(s, s).wait_recv())
    for c in range(copies):
        for j in range(HEADS // 2):
            one, two = call[c * HEADS + 2 * j], call[c * HEADS + 2 * j + 1]
            r0, cols = c * share, slice(j * PAIR, (j + 1) * PAIR)
            ctx[r0 : r0 + half, cols] = jnp.concatenate([one[:, :DH], two[:, :DH]], axis=1)
            ctx[r0 + half : r0 + share, cols] = jnp.concatenate([one[:, DH:], two[:, DH:]], axis=1)

    mates = mate % plane

    def take_b(z):
        for g in range(groups):
            for side in range(2):
                b_copy(z, side, g, mates).wait_recv()

    whole_copy(0, mates).wait_recv()
    for g in range(groups):
        b_copy(zed, 1, g, mates).wait_recv()
    beyond(take_b)
    for d in range(0, n, 2):
        pair = jnp.concatenate([wall[d], wall[d + 1]], axis=1)
        o_ref[:, d * width : (d + 2) * width] = jnp.dot(
            ctx[...], pair, preferred_element_type=jnp.float32
        ).astype(bf16)

    def sent(d):
        q_copy(d, me).wait_send()
        kv_copy(d, me).wait_send()
        c_copy(d, me).wait_send()

    others(sent)

    def sent_layer(z):
        relay(z, lambda copy: copy.wait_send())
        y_copy(z, spot, over).wait_send()
        for side in range(2):
            for g in range(1, groups):
                x_copy(z, side, g, grp).wait_send()
            for g in range(groups):
                b_copy(z, side, g, spot).wait_send()

    beyond(sent_layer)
    hop(lambda copy: copy.wait_send(), False)
    hop(lambda copy: copy.wait_send(), True)
    y_copy(zed, spot, over, True).wait_send()
    for g in range(1, groups):
        x_copy(zed, 1, g, grp).wait_send()
        b_copy(zed, 1, g, spot).wait_send()
    b_copy(zed, 1, 0, spot).wait_send()
    whole_copy(0, spot).wait_send()


def per_device(groups, n, queries, encoder_rows, key_weight, value_weight, out_weight):
    rows, wide = queries.shape
    enc, model = encoder_rows.shape
    depth, width = out_weight.shape
    plane = math.gcd(n, 4)
    layers = n // plane
    chunks = 4
    half = rows // (n // HEADS) // 2
    bf16 = jnp.bfloat16
    dma = lambda k: pltpu.SemaphoreType.DMA((k,))
    hbm = pl.BlockSpec(memory_space=pl.ANY)
    return pl.pallas_call(
        functools.partial(kernel, groups, n, plane, chunks),
        out_shape=pltpu.VMEM((rows, n * width), bf16),
        in_specs=[hbm] * 5,
        out_specs=pl.BlockSpec(memory_space=pltpu.VMEM),
        scratch_shapes=[
            pltpu.VMEM((rows, wide), bf16),
            pltpu.VMEM((enc, model), bf16),
            pltpu.VMEM((chunks, model, wide // chunks), bf16),
            pltpu.VMEM((chunks, model, wide // chunks), bf16),
            pltpu.VMEM((n, half, PAIR), bf16),
            pltpu.VMEM((HEADS, enc, PAIR), bf16),
            pltpu.VMEM((n, half, PAIR), bf16),
            pltpu.VMEM((n * enc, PAIR), bf16),
            pltpu.VMEM((2, n * enc, PAIR), bf16),
            pltpu.VMEM((2, n * enc, PAIR), bf16),
            pltpu.VMEM((n, half, PAIR), bf16),
            pltpu.VMEM((n, half, PAIR), bf16),
            pltpu.VMEM((rows, depth), bf16),
            pltpu.VMEM((n, depth, width), bf16),
            dma(2 * chunks),
            dma(3),
            dma(n), dma(n), dma(n), dma(n), dma(n), dma(n),
            dma(layers * layers), dma(layers), dma(layers), dma(layers),
            dma(2 * groups * layers), dma(2 * groups * layers),
            dma(2 * groups * layers), dma(2 * groups * layers),
        ],
        compiler_params=pltpu.CompilerParams(
            collective_id=0, has_side_effects=True, vmem_limit_bytes=56 * 1024 * 1024
        ),
    )(queries, encoder_rows, key_weight, value_weight, out_weight)


def solution(mesh):
    groups, n = mesh.shape["groups"], mesh.shape["ctx"]
    return jax.shard_map(
        functools.partial(per_device, groups, n),
        mesh=mesh,
        in_specs=(P(("groups", "ctx"), None), P(("groups", "ctx"), None), P(), P(), P(None, "ctx")),
        out_specs=P(("groups", "ctx"), None),
        check_vma=False,
    )
```

```python
import functools
import math

import jax
import jax.numpy as jnp
from jax import lax
from jax.experimental import pallas as pl
from jax.experimental.pallas import tpu as pltpu
from jax.sharding import PartitionSpec as P

HEADS = 16
DH = 64
PAIR = 2 * DH
MESH = pl.DeviceIdType.MESH
LOG2E = 1.4426950408889634
ORDER = (
    "o", "n", "p0", "p1", "p2", "p3", "Q", "q0", "z1", "f", "y0", "r1",
    "q3", "q2", "q1", "y1", "z2", "r2", "K", "a0", "x1", "x0", "y2", "a1",
    "z3", "a2", "a3", "y3", "x2", "x3",
)


def kernel(
    groups, n, plane, chunks,
    q_hbm, e_hbm, kw_hbm, vw_hbm, ow_hbm, o_ref,
    q_ref, e_ref, kw, vw, qpack, kvpack, qall, kvall, keys2, vals2, cpack, call, ctx, wall,
    load_sem, own_sem, q_send, q_recv, kv_send, kv_recv, c_send, c_recv,
    z_send, z_recv, y_send, y_recv, x_send, x_recv, b_send, b_recv,
):
    grp = lax.axis_index("groups")
    me = lax.axis_index("ctx")
    rows = q_ref.shape[0]
    enc = e_ref.shape[0]
    depth = wall.shape[1]
    width = wall.shape[2]
    copies = n // HEADS
    share = rows // copies
    half = share // 2
    part = depth // groups
    layers = n // plane
    zed = me // plane
    spot = me % plane
    far = plane // 2
    over = zed * plane + (spot + far) % plane
    mate = zed * plane + (spot // 2) * 2 + (1 - spot % 2)
    heads = HEADS // chunks
    bf16 = jnp.bfloat16

    barrier = pltpu.get_barrier_semaphore()

    def greet(i, carry):
        pl.semaphore_signal(
            barrier, inc=1, device_id=(grp, (me + i) % n), device_id_type=MESH
        )
        return carry

    lax.fori_loop(1, n, greet, 0)
    for g in range(1, groups):
        pl.semaphore_signal(
            barrier, inc=1, device_id=((grp + g) % groups, me), device_id_type=MESH
        )

    load_q = pltpu.make_async_copy(q_hbm, q_ref, own_sem.at[0])
    load_w = pltpu.make_async_copy(ow_hbm, wall.at[me], own_sem.at[1])
    load_e = pltpu.make_async_copy(e_hbm, e_ref, own_sem.at[2])
    offsets = sorted(range(chunks), key=lambda i: (-min(i, chunks - i), i))

    def chunk_at(i):
        return (zed + offsets[i]) % chunks

    def loads(i):
        wide = kw.shape[2]
        cols = pl.ds(pl.multiple_of(chunk_at(i) * wide, wide), wide)
        return (
            pltpu.make_async_copy(kw_hbm.at[:, cols], kw.at[i], load_sem.at[i]),
            pltpu.make_async_copy(vw_hbm.at[:, cols], vw.at[i], load_sem.at[chunks + i]),
        )

    load_e.start()
    for i in range(chunks):
        for copy in loads(i):
            copy.start()
        if i == 0:
            load_q.start()
            load_w.start()

    def remote(src, dst, send, recv, to):
        return pltpu.make_async_remote_copy(
            src_ref=src, dst_ref=dst, send_sem=send, recv_sem=recv,
            device_id=to, device_id_type=MESH,
        )

    def q_copy(d, s):
        return remote(qpack.at[d], qall.at[s], q_send.at[d], q_recv.at[s], (grp, d))

    def kv_copy(d, s):
        return remote(
            kvpack.at[d % HEADS], kvall.at[pl.ds(s * enc, enc)],
            kv_send.at[d], kv_recv.at[s], (grp, d),
        )

    def c_copy(d, s):
        return remote(cpack.at[d], call.at[s], c_send.at[d], c_recv.at[s], (grp, d))

    mine = pl.ds(grp * part, part)

    def z_copy(src, to, own=False):
        block = wall.at[src * plane + spot, mine]
        return remote(
            ow_hbm.at[mine] if own else block, block, z_send.at[src * layers + to], z_recv.at[src],
            (grp, to * plane + spot),
        )

    middle = layers // 2

    def hop(act, across):
        for to in range(layers):
            if across:
                near = ((zed < middle - 1) & (to == middle)) | ((zed > middle) & (to == middle - 1))
            else:
                near = ((zed < middle) & ((to < middle) | ((to == middle) & (zed == middle - 1)))) | (
                    (zed >= middle) & ((to >= middle) | ((to == middle - 1) & (zed == middle)))
                )

            @pl.when(near & (zed != to))
            def _(to=to):
                act(z_copy(zed, to, True))

    def relay(src, act):
        for to in range(layers):
            if to > middle:

                @pl.when((zed == middle) & (src < middle))
                def _(to=to):
                    act(z_copy(src, to))

            if to < middle - 1:

                @pl.when((zed == middle - 1) & (src >= middle))
                def _(to=to):
                    act(z_copy(src, to))

    def y_copy(layer, at, to, own=False):
        block = wall.at[layer * plane + at, mine]
        return remote(ow_hbm.at[mine] if own else block, block, y_send.at[layer], y_recv.at[layer], (grp, to))

    def x_copy(layer, side, g, whose):
        at = layer * plane + (spot + side * far) % plane
        block = wall.at[at, pl.ds(whose * part, part)]
        slot = (g * 2 + side) * layers + layer
        return remote(
            block, block, x_send.at[slot], x_recv.at[slot], ((grp + g) % groups, me)
        )

    def b_copy(layer, side, g, at):
        whose = (grp + groups - g) % groups
        block = wall.at[layer * plane + (at + side * far) % plane, pl.ds(whose * part, part)]
        slot = (g * 2 + side) * layers + layer
        return remote(block, block, b_send.at[slot], b_recv.at[slot], (grp, mate))

    def whole_copy(side, at):
        block = wall.at[zed * plane + (at + side * far) % plane]
        slot = side * layers + zed
        return remote(ow_hbm, block, b_send.at[slot], b_recv.at[slot], (grp, mate))

    def some(first, last, body):
        def step(i, carry):
            body((me + i) % n)
            return carry

        lax.fori_loop(first, last, step, 0)

    def others(body):
        some(1, n, body)

    def beyond(body):
        def step(i, carry):
            body((zed + i) % layers)
            return carry

        lax.fori_loop(1, layers, step, 0)

    def far_first(body):
        def step(i, carry):
            d = (me + n // 2 + i) % n

            @pl.when(d != me)
            def _():
                body(d)

            return carry

        lax.fori_loop(0, n, step, 0)

    def sources(k, body):
        for src in (zed - k, zed + k):

            @pl.when((src >= 0) & (src < layers))
            def _(src=src):
                body(src)

    def on_z(src):
        z_copy(src, zed).wait_recv()
        y_copy(src, spot, over).start()
        for g in range(1, groups):
            x_copy(src, 0, g, grp).start()
        b_copy(src, 0, 0, spot).start()

    def on_y(src):
        y_copy(src, (spot + far) % plane, over).wait_recv()
        for g in range(1, groups):
            x_copy(src, 1, g, grp).start()
        b_copy(src, 1, 0, spot).start()

    def on_x(src):
        for g in range(1, groups):
            for side in range(2):
                x_copy(src, side, g, (grp + groups - g) % groups).wait_recv()
                b_copy(src, side, g, spot).start()

    def on_far(src):
        for g in range(1, groups):
            x_copy(src, 1, g, (grp + groups - g) % groups).wait_recv()
            b_copy(src, 1, g, spot).start()

    events = {"y0": lambda: on_y(zed), "x0": lambda: on_far(zed)}
    for k in range(1, layers):
        events[f"z{k}"] = functools.partial(sources, k, on_z)
        events[f"r{k}"] = functools.partial(sources, k, lambda src: relay(src, lambda copy: copy.start()))
        events[f"y{k}"] = functools.partial(sources, k, on_y)
        events[f"x{k}"] = functools.partial(sources, k, on_x)

    pl.semaphore_wait(barrier, n - 1 + groups - 1)
    def pack_q():
        load_q.wait()
        for d in range(n):
            r0, c0 = (d // HEADS) * share, (d % HEADS) * DH
            qpack[d] = jnp.concatenate(
                [q_ref[r0 : r0 + half, c0 : c0 + DH], q_ref[r0 + half : r0 + share, c0 : c0 + DH]],
                axis=1,
            )
        qall[me] = qpack[me]

    def start_own():
        hop(lambda copy: copy.start(), False)

    def start_across():
        hop(lambda copy: copy.start(), True)

    def start_near():
        y_copy(zed, spot, over, True).start()
        whole_copy(0, spot).start()

    def project(i):
        if i == 0:
            load_e.wait()
        one, two = loads(i)
        one.wait()
        two.wait()
        j = chunk_at(i)
        keys = jnp.dot(e_ref[...], kw[i], preferred_element_type=jnp.float32).astype(bf16)
        values = jnp.dot(e_ref[...], vw[i], preferred_element_type=jnp.float32).astype(bf16)
        for h in range(heads):
            cols = slice(h * DH, (h + 1) * DH)
            kvpack[j * heads + h] = jnp.concatenate([keys[:, cols], values[:, cols]], axis=1)

    def send_kv(i):
        j = chunk_at(i)
        for c in range(copies):
            for h in range(heads):
                d = c * HEADS + j * heads + (h + spot) % heads

                @pl.when(d != me)
                def _(d=d):
                    kv_copy(d, me).start()

    def project_and_send(i):
        project(i)
        send_kv(i)

    def apart(k):
        at, bit = me, 1
        while bit <= k:
            if k & bit:
                at = at + bit * (1 - 2 * (me // bit % 2))
            bit *= 2
        return at

    def send_q(first, last):
        for k in range(last - 1, first - 1, -1):
            if k:
                q_copy(apart(k), me).start()

    def take_kv():
        kvall[pl.ds(me * enc, enc)] = kvpack[me % HEADS]
        others(lambda s: kv_copy(s, s).wait_recv())
        memory = kvall[...]
        nothing, ones = jnp.zeros((n * enc, DH), bf16), jnp.ones((n * enc, DH), bf16)
        keys2[0] = jnp.concatenate([memory[:, :DH], nothing], axis=1)
        keys2[1] = jnp.concatenate([nothing, memory[:, :DH]], axis=1)
        vals2[0] = jnp.concatenate([memory[:, DH:], ones], axis=1)
        vals2[1] = jnp.concatenate([ones, memory[:, DH:]], axis=1)

    together = min(n, max(1, 256 // half))
    left = lax.broadcasted_iota(jnp.int32, (together * half, PAIR), 1) < DH

    steps = n // together

    def attend(i):
        whose = [apart(k) for k in range(i * together, (i + 1) * together)]
        for k, s in zip(range(i * together, (i + 1) * together), whose):
            if k:
                q_copy(s, s).wait_recv()

        query = jnp.concatenate([qall[s] for s in whose], axis=0)
        summed = []
        for side in range(2):
            scores = lax.dot_general(
                query, keys2[side], (((1,), (1,)), ((), ())), preferred_element_type=jnp.float32
            )
            top = jnp.max(scores, axis=1, keepdims=True)
            expo = jnp.exp2((scores - top) * (0.125 * LOG2E)).astype(bf16)
            summed.append(jnp.dot(expo, vals2[side], preferred_element_type=jnp.float32))
        over_total = jnp.where(left, summed[1], summed[0])
        out = (jnp.where(left, summed[0], summed[1]) / pltpu.roll(over_total, DH, 1)).astype(bf16)
        for j, s in enumerate(whose):
            cpack[s] = out[j * half : (j + 1) * half]
        return whose

    def send(whose):
        for s in whose:

            @pl.when(s != me)
            def _(s=s):
                c_copy(s, me).start()


    def turn(i):
        send(attend(i))

    steps = n // together
    acts = dict(events)
    acts["Q"] = pack_q
    acts["o"], acts["n"], acts["K"], acts["f"] = start_own, start_near, take_kv, start_across
    for i in range(chunks):
        acts[f"p{i}"] = functools.partial(project_and_send, i)
        acts[f"c{i}"] = functools.partial(project, i)
        acts[f"s{i}"] = functools.partial(send_kv, i)
    for i in range(4):
        acts[f"q{i}"] = functools.partial(send_q, n * i // 4, n * (i + 1) // 4)
    for i in range(steps):
        acts[f"a{i}"] = functools.partial(turn, i)
    rest = [f"a{i}" for i in range(steps)]
    for k in range(1, layers):
        rest += [f"z{k}", f"r{k}", f"y{k}", f"x{k}"]
    known = [name for name in ORDER if name in acts]
    for name in known + [name for name in rest if name not in known]:
        acts[name]()

    load_w.wait()
    call[me] = cpack[me]
    others(lambda s: c_copy(s, s).wait_recv())
    for c in range(copies):
        for j in range(HEADS // 2):
            one, two = call[c * HEADS + 2 * j], call[c * HEADS + 2 * j + 1]
            r0, cols = c * share, slice(j * PAIR, (j + 1) * PAIR)
            ctx[r0 : r0 + half, cols] = jnp.concatenate([one[:, :DH], two[:, :DH]], axis=1)
            ctx[r0 + half : r0 + share, cols] = jnp.concatenate([one[:, DH:], two[:, DH:]], axis=1)

    mates = mate % plane

    def take_b(z):
        for g in range(groups):
            for side in range(2):
                b_copy(z, side, g, mates).wait_recv()

    whole_copy(0, mates).wait_recv()
    for g in range(groups):
        b_copy(zed, 1, g, mates).wait_recv()
    beyond(take_b)
    for d in range(0, n, 2):
        pair = jnp.concatenate([wall[d], wall[d + 1]], axis=1)
        o_ref[:, d * width : (d + 2) * width] = jnp.dot(
            ctx[...], pair, preferred_element_type=jnp.float32
        ).astype(bf16)

    def sent(d):
        q_copy(d, me).wait_send()
        kv_copy(d, me).wait_send()
        c_copy(d, me).wait_send()

    others(sent)

    def sent_layer(z):
        relay(z, lambda copy: copy.wait_send())
        y_copy(z, spot, over).wait_send()
        for side in range(2):
            for g in range(1, groups):
                x_copy(z, side, g, grp).wait_send()
            for g in range(groups):
                b_copy(z, side, g, spot).wait_send()

    beyond(sent_layer)
    hop(lambda copy: copy.wait_send(), False)
    hop(lambda copy: copy.wait_send(), True)
    y_copy(zed, spot, over, True).wait_send()
    for g in range(1, groups):
        x_copy(zed, 1, g, grp).wait_send()
        b_copy(zed, 1, g, spot).wait_send()
    b_copy(zed, 1, 0, spot).wait_send()
    whole_copy(0, spot).wait_send()


def per_device(groups, n, queries, encoder_rows, key_weight, value_weight, out_weight):
    rows, wide = queries.shape
    enc, model = encoder_rows.shape
    depth, width = out_weight.shape
    plane = math.gcd(n, 4)
    layers = n // plane
    chunks = 4
    half = rows // (n // HEADS) // 2
    bf16 = jnp.bfloat16
    dma = lambda k: pltpu.SemaphoreType.DMA((k,))
    hbm = pl.BlockSpec(memory_space=pl.ANY)
    return pl.pallas_call(
        functools.partial(kernel, groups, n, plane, chunks),
        out_shape=pltpu.VMEM((rows, n * width), bf16),
        in_specs=[hbm] * 5,
        out_specs=pl.BlockSpec(memory_space=pltpu.VMEM),
        scratch_shapes=[
            pltpu.VMEM((rows, wide), bf16),
            pltpu.VMEM((enc, model), bf16),
            pltpu.VMEM((chunks, model, wide // chunks), bf16),
            pltpu.VMEM((chunks, model, wide // chunks), bf16),
            pltpu.VMEM((n, half, PAIR), bf16),
            pltpu.VMEM((HEADS, enc, PAIR), bf16),
            pltpu.VMEM((n, half, PAIR), bf16),
            pltpu.VMEM((n * enc, PAIR), bf16),
            pltpu.VMEM((2, n * enc, PAIR), bf16),
            pltpu.VMEM((2, n * enc, PAIR), bf16),
            pltpu.VMEM((n, half, PAIR), bf16),
            pltpu.VMEM((n, half, PAIR), bf16),
            pltpu.VMEM((rows, depth), bf16),
            pltpu.VMEM((n, depth, width), bf16),
            dma(2 * chunks),
            dma(3),
            dma(n), dma(n), dma(n), dma(n), dma(n), dma(n),
            dma(layers * layers), dma(layers), dma(layers), dma(layers),
            dma(2 * groups * layers), dma(2 * groups * layers),
            dma(2 * groups * layers), dma(2 * groups * layers),
        ],
        compiler_params=pltpu.CompilerParams(
            collective_id=0, has_side_effects=True, vmem_limit_bytes=56 * 1024 * 1024
        ),
    )(queries, encoder_rows, key_weight, value_weight, out_weight)


def solution(mesh):
    groups, n = mesh.shape["groups"], mesh.shape["ctx"]
    return jax.shard_map(
        functools.partial(per_device, groups, n),
        mesh=mesh,
        in_specs=(P(("groups", "ctx"), None), P(("groups", "ctx"), None), P(), P(), P(None, "ctx")),
        out_specs=P(("groups", "ctx"), None),
        check_vma=False,
    )
```

```python
import functools
import math

import jax
import jax.numpy as jnp
from jax import lax
from jax.experimental import pallas as pl
from jax.experimental.pallas import tpu as pltpu
from jax.sharding import PartitionSpec as P

HEADS = 16
DH = 64
PAIR = 2 * DH
MESH = pl.DeviceIdType.MESH
LOG2E = 1.4426950408889634
ORDER = (
    "o", "n", "p0", "p1", "p2", "p3", "Q", "q0", "z1", "f", "y0", "r1",
    "q3", "q2", "q1", "y1", "z2", "r2", "K", "a0", "x1", "x0", "y2", "a1",
    "z3", "a2", "a3", "y3", "x2", "x3",
)


def kernel(
    groups, n, plane, chunks,
    q_hbm, e_hbm, kw_hbm, vw_hbm, ow_hbm, o_ref,
    q_ref, e_ref, kw, vw, qpack, kvpack, qall, kvall, keys2, vals2, cpack, call, ctx, total, wall,
    load_sem, own_sem, q_send, q_recv, kv_send, kv_recv, c_send, c_recv,
    z_send, z_recv, y_send, y_recv, x_send, x_recv, b_send, b_recv,
):
    grp = lax.axis_index("groups")
    me = lax.axis_index("ctx")
    rows = q_ref.shape[0]
    enc = e_ref.shape[0]
    depth = wall.shape[1]
    width = wall.shape[2]
    copies = n // HEADS
    share = rows // copies
    half = share // 2
    part = depth // groups
    layers = n // plane
    zed = me // plane
    spot = me % plane
    far = plane // 2
    over = zed * plane + (spot + far) % plane
    mate = zed * plane + (spot // 2) * 2 + (1 - spot % 2)
    heads = HEADS // chunks
    bf16 = jnp.bfloat16

    barrier = pltpu.get_barrier_semaphore()

    def greet(i, carry):
        pl.semaphore_signal(
            barrier, inc=1, device_id=(grp, (me + i) % n), device_id_type=MESH
        )
        return carry

    lax.fori_loop(1, n, greet, 0)
    for g in range(1, groups):
        pl.semaphore_signal(
            barrier, inc=1, device_id=((grp + g) % groups, me), device_id_type=MESH
        )

    load_q = pltpu.make_async_copy(q_hbm, q_ref, own_sem.at[0])
    load_w = pltpu.make_async_copy(ow_hbm, wall.at[me], own_sem.at[1])
    load_e = pltpu.make_async_copy(e_hbm, e_ref, own_sem.at[2])
    offsets = sorted(range(chunks), key=lambda i: (-min(i, chunks - i), i))

    def chunk_at(i):
        return (zed + offsets[i]) % chunks

    def loads(i):
        wide = kw.shape[2]
        cols = pl.ds(pl.multiple_of(chunk_at(i) * wide, wide), wide)
        return (
            pltpu.make_async_copy(kw_hbm.at[:, cols], kw.at[i], load_sem.at[i]),
            pltpu.make_async_copy(vw_hbm.at[:, cols], vw.at[i], load_sem.at[chunks + i]),
        )

    load_e.start()
    for i in range(chunks):
        for copy in loads(i):
            copy.start()
        if i == 0:
            load_q.start()
            load_w.start()

    def remote(src, dst, send, recv, to):
        return pltpu.make_async_remote_copy(
            src_ref=src, dst_ref=dst, send_sem=send, recv_sem=recv,
            device_id=to, device_id_type=MESH,
        )

    def q_copy(d, s):
        return remote(qpack.at[d], qall.at[s], q_send.at[d], q_recv.at[s], (grp, d))

    def kv_copy(d, s):
        return remote(
            kvpack.at[d % HEADS], kvall.at[pl.ds(s * enc, enc)],
            kv_send.at[d], kv_recv.at[s], (grp, d),
        )

    def c_copy(d, s):
        return remote(cpack.at[d], call.at[s], c_send.at[d], c_recv.at[s], (grp, d))

    mine = pl.ds(grp * part, part)

    def z_copy(src, to, own=False):
        block = wall.at[src * plane + spot, mine]
        return remote(
            ow_hbm.at[mine] if own else block, block, z_send.at[src * layers + to], z_recv.at[src],
            (grp, to * plane + spot),
        )

    middle = layers // 2

    def hop(act, across):
        for to in range(layers):
            if across:
                near = ((zed < middle - 1) & (to == middle)) | ((zed > middle) & (to == middle - 1))
            else:
                near = ((zed < middle) & ((to < middle) | ((to == middle) & (zed == middle - 1)))) | (
                    (zed >= middle) & ((to >= middle) | ((to == middle - 1) & (zed == middle)))
                )

            @pl.when(near & (zed != to))
            def _(to=to):
                act(z_copy(zed, to, True))

    def relay(src, act):
        for to in range(layers):
            if to > middle:

                @pl.when((zed == middle) & (src < middle))
                def _(to=to):
                    act(z_copy(src, to))

            if to < middle - 1:

                @pl.when((zed == middle - 1) & (src >= middle))
                def _(to=to):
                    act(z_copy(src, to))

    def y_copy(layer, at, to, own=False):
        block = wall.at[layer * plane + at, mine]
        return remote(ow_hbm.at[mine] if own else block, block, y_send.at[layer], y_recv.at[layer], (grp, to))

    def x_copy(layer, side, g, whose):
        at = layer * plane + (spot + side * far) % plane
        block = wall.at[at, pl.ds(whose * part, part)]
        slot = (g * 2 + side) * layers + layer
        return remote(
            block, block, x_send.at[slot], x_recv.at[slot], ((grp + g) % groups, me)
        )

    def b_copy(layer, side, g, at):
        whose = (grp + groups - g) % groups
        block = wall.at[layer * plane + (at + side * far) % plane, pl.ds(whose * part, part)]
        slot = (g * 2 + side) * layers + layer
        return remote(block, block, b_send.at[slot], b_recv.at[slot], (grp, mate))

    def whole_copy(side, at):
        block = wall.at[zed * plane + (at + side * far) % plane]
        slot = side * layers + zed
        return remote(ow_hbm, block, b_send.at[slot], b_recv.at[slot], (grp, mate))

    def some(first, last, body):
        def step(i, carry):
            body((me + i) % n)
            return carry

        lax.fori_loop(first, last, step, 0)

    def others(body):
        some(1, n, body)

    def beyond(body):
        def step(i, carry):
            body((zed + i) % layers)
            return carry

        lax.fori_loop(1, layers, step, 0)

    def far_first(body):
        def step(i, carry):
            d = (me + n // 2 + i) % n

            @pl.when(d != me)
            def _():
                body(d)

            return carry

        lax.fori_loop(0, n, step, 0)

    def sources(k, body):
        for src in (zed - k, zed + k):

            @pl.when((src >= 0) & (src < layers))
            def _(src=src):
                body(src)

    def on_z(src):
        z_copy(src, zed).wait_recv()
        y_copy(src, spot, over).start()
        for g in range(1, groups):
            x_copy(src, 0, g, grp).start()
        b_copy(src, 0, 0, spot).start()

    def on_y(src):
        y_copy(src, (spot + far) % plane, over).wait_recv()
        for g in range(1, groups):
            x_copy(src, 1, g, grp).start()
        b_copy(src, 1, 0, spot).start()

    def on_x(src):
        for g in range(1, groups):
            for side in range(2):
                x_copy(src, side, g, (grp + groups - g) % groups).wait_recv()
                b_copy(src, side, g, spot).start()

    def on_far(src):
        for g in range(1, groups):
            x_copy(src, 1, g, (grp + groups - g) % groups).wait_recv()
            b_copy(src, 1, g, spot).start()

    events = {"y0": lambda: on_y(zed), "x0": lambda: on_far(zed)}
    for k in range(1, layers):
        events[f"z{k}"] = functools.partial(sources, k, on_z)
        events[f"r{k}"] = functools.partial(sources, k, lambda src: relay(src, lambda copy: copy.start()))
        events[f"y{k}"] = functools.partial(sources, k, on_y)
        events[f"x{k}"] = functools.partial(sources, k, on_x)

    pl.semaphore_wait(barrier, n - 1 + groups - 1)
    def pack_q():
        load_q.wait()
        for d in range(n):
            r0, c0 = (d // HEADS) * share, (d % HEADS) * DH
            qpack[d] = jnp.concatenate(
                [q_ref[r0 : r0 + half, c0 : c0 + DH], q_ref[r0 + half : r0 + share, c0 : c0 + DH]],
                axis=1,
            )
        qall[me] = qpack[me]

    def start_own():
        hop(lambda copy: copy.start(), False)

    def start_across():
        hop(lambda copy: copy.start(), True)

    def start_near():
        y_copy(zed, spot, over, True).start()
        whole_copy(0, spot).start()

    def project(i):
        if i == 0:
            load_e.wait()
        one, two = loads(i)
        one.wait()
        two.wait()
        j = chunk_at(i)
        keys = jnp.dot(e_ref[...], kw[i], preferred_element_type=jnp.float32).astype(bf16)
        values = jnp.dot(e_ref[...], vw[i], preferred_element_type=jnp.float32).astype(bf16)
        for h in range(heads):
            cols = slice(h * DH, (h + 1) * DH)
            kvpack[j * heads + h] = jnp.concatenate([keys[:, cols], values[:, cols]], axis=1)

    def send_kv(i):
        j = chunk_at(i)
        for c in range(copies):
            for h in range(heads):
                d = c * HEADS + j * heads + (h + spot) % heads

                @pl.when(d != me)
                def _(d=d):
                    kv_copy(d, me).start()

    def project_and_send(i):
        project(i)
        send_kv(i)

    def apart(k):
        at, bit = me, 1
        while bit <= k:
            if k & bit:
                at = at + bit * (1 - 2 * (me // bit % 2))
            bit *= 2
        return at

    def send_q(first, last):
        for k in range(last - 1, first - 1, -1):
            if k:
                q_copy(apart(k), me).start()

    def take_kv():
        kvall[pl.ds(me * enc, enc)] = kvpack[me % HEADS]
        others(lambda s: kv_copy(s, s).wait_recv())
        memory = kvall[...]
        nothing, ones = jnp.zeros((n * enc, DH), bf16), jnp.ones((n * enc, DH), bf16)
        keys2[0] = jnp.concatenate([memory[:, :DH], nothing], axis=1)
        keys2[1] = jnp.concatenate([nothing, memory[:, :DH]], axis=1)
        vals2[0] = jnp.concatenate([memory[:, DH:], ones], axis=1)
        vals2[1] = jnp.concatenate([ones, memory[:, DH:]], axis=1)

    together = min(n, max(1, 256 // half))
    left = lax.broadcasted_iota(jnp.int32, (together * half, PAIR), 1) < DH

    steps = n // together

    def attend(i):
        whose = [apart(k) for k in range(i * together, (i + 1) * together)]
        for k, s in zip(range(i * together, (i + 1) * together), whose):
            if k:
                q_copy(s, s).wait_recv()

        query = jnp.concatenate([qall[s] for s in whose], axis=0)
        summed = []
        for side in range(2):
            scores = lax.dot_general(
                query, keys2[side], (((1,), (1,)), ((), ())), preferred_element_type=jnp.float32
            )
            top = jnp.max(scores, axis=1, keepdims=True)
            expo = jnp.exp2((scores - top) * (0.125 * LOG2E)).astype(bf16)
            summed.append(jnp.dot(expo, vals2[side], preferred_element_type=jnp.float32))
        over_total = jnp.where(left, summed[1], summed[0])
        out = (jnp.where(left, summed[0], summed[1]) / pltpu.roll(over_total, DH, 1)).astype(bf16)
        for j, s in enumerate(whose):
            cpack[s] = out[j * half : (j + 1) * half]
        return whose

    def send(whose):
        for s in whose:

            @pl.when(s != me)
            def _(s=s):
                c_copy(s, me).start()


    def turn(i):
        send(attend(i))

    steps = n // together
    acts = dict(events)
    acts["Q"] = pack_q
    acts["o"], acts["n"], acts["K"], acts["f"] = start_own, start_near, take_kv, start_across
    for i in range(chunks):
        acts[f"p{i}"] = functools.partial(project_and_send, i)
        acts[f"c{i}"] = functools.partial(project, i)
        acts[f"s{i}"] = functools.partial(send_kv, i)
    for i in range(4):
        acts[f"q{i}"] = functools.partial(send_q, n * i // 4, n * (i + 1) // 4)
    for i in range(steps):
        acts[f"a{i}"] = functools.partial(turn, i)
    rest = [f"a{i}" for i in range(steps)]
    for k in range(1, layers):
        rest += [f"z{k}", f"r{k}", f"y{k}", f"x{k}"]
    known = [name for name in ORDER if name in acts]
    for name in known + [name for name in rest if name not in known]:
        acts[name]()

    load_w.wait()
    call[me] = cpack[me]
    mates = mate % plane

    def take_b(z):
        for g in range(groups):
            for side in range(2):
                b_copy(z, side, g, mates).wait_recv()

    whole_copy(0, mates).wait_recv()
    for g in range(groups):
        b_copy(zed, 1, g, mates).wait_recv()
    beyond(take_b)
    near = n // 2
    base = me // near * near

    def unpack(at):
        for j in range(0, near, 2):
            one, two = call[at + j], call[at + j + 1]
            cols = pl.ds(pl.multiple_of((at + j) * DH, PAIR), PAIR)
            ctx[:half, cols] = jnp.concatenate([one[:, :DH], two[:, :DH]], axis=1)
            ctx[half:, cols] = jnp.concatenate([one[:, DH:], two[:, DH:]], axis=1)

    def product(at, d):
        heads_at = pl.ds(pl.multiple_of(at * DH, near * DH), near * DH)
        pair = jnp.concatenate([wall[d, heads_at], wall[d + 1, heads_at]], axis=1)
        return jnp.dot(ctx[:, heads_at], pair, preferred_element_type=jnp.float32)

    if copies == 1:
        for k in range(1, near):
            c_copy(apart(k), apart(k)).wait_recv()
        unpack(base)
        for d in range(0, n, 2):
            total[:, d * width : (d + 2) * width] = product(base, d)
        for k in range(near, n):
            c_copy(apart(k), apart(k)).wait_recv()
        unpack(near - base)
        for d in range(0, n, 2):
            cols = slice(d * width, (d + 2) * width)
            o_ref[:, cols] = (total[:, cols] + product(near - base, d)).astype(bf16)
    else:
        others(lambda s: c_copy(s, s).wait_recv())
        for c in range(copies):
            for j in range(HEADS // 2):
                one, two = call[c * HEADS + 2 * j], call[c * HEADS + 2 * j + 1]
                r0, cols = c * share, slice(j * PAIR, (j + 1) * PAIR)
                ctx[r0 : r0 + half, cols] = jnp.concatenate([one[:, :DH], two[:, :DH]], axis=1)
                ctx[r0 + half : r0 + share, cols] = jnp.concatenate([one[:, DH:], two[:, DH:]], axis=1)
        for d in range(0, n, 2):
            pair = jnp.concatenate([wall[d], wall[d + 1]], axis=1)
            o_ref[:, d * width : (d + 2) * width] = jnp.dot(
                ctx[...], pair, preferred_element_type=jnp.float32
            ).astype(bf16)

    def sent(d):
        q_copy(d, me).wait_send()
        kv_copy(d, me).wait_send()
        c_copy(d, me).wait_send()

    others(sent)

    def sent_layer(z):
        relay(z, lambda copy: copy.wait_send())
        y_copy(z, spot, over).wait_send()
        for side in range(2):
            for g in range(1, groups):
                x_copy(z, side, g, grp).wait_send()
            for g in range(groups):
                b_copy(z, side, g, spot).wait_send()

    beyond(sent_layer)
    hop(lambda copy: copy.wait_send(), False)
    hop(lambda copy: copy.wait_send(), True)
    y_copy(zed, spot, over, True).wait_send()
    for g in range(1, groups):
        x_copy(zed, 1, g, grp).wait_send()
        b_copy(zed, 1, g, spot).wait_send()
    b_copy(zed, 1, 0, spot).wait_send()
    whole_copy(0, spot).wait_send()


def per_device(groups, n, queries, encoder_rows, key_weight, value_weight, out_weight):
    rows, wide = queries.shape
    enc, model = encoder_rows.shape
    depth, width = out_weight.shape
    plane = math.gcd(n, 4)
    layers = n // plane
    chunks = 4
    half = rows // (n // HEADS) // 2
    bf16 = jnp.bfloat16
    dma = lambda k: pltpu.SemaphoreType.DMA((k,))
    hbm = pl.BlockSpec(memory_space=pl.ANY)
    return pl.pallas_call(
        functools.partial(kernel, groups, n, plane, chunks),
        out_shape=pltpu.VMEM((rows, n * width), bf16),
        in_specs=[hbm] * 5,
        out_specs=pl.BlockSpec(memory_space=pltpu.VMEM),
        scratch_shapes=[
            pltpu.VMEM((rows, wide), bf16),
            pltpu.VMEM((enc, model), bf16),
            pltpu.VMEM((chunks, model, wide // chunks), bf16),
            pltpu.VMEM((chunks, model, wide // chunks), bf16),
            pltpu.VMEM((n, half, PAIR), bf16),
            pltpu.VMEM((HEADS, enc, PAIR), bf16),
            pltpu.VMEM((n, half, PAIR), bf16),
            pltpu.VMEM((n * enc, PAIR), bf16),
            pltpu.VMEM((2, n * enc, PAIR), bf16),
            pltpu.VMEM((2, n * enc, PAIR), bf16),
            pltpu.VMEM((n, half, PAIR), bf16),
            pltpu.VMEM((n, half, PAIR), bf16),
            pltpu.VMEM((rows, depth), bf16),
            pltpu.VMEM((rows, n * width), jnp.float32),
            pltpu.VMEM((n, depth, width), bf16),
            dma(2 * chunks),
            dma(3),
            dma(n), dma(n), dma(n), dma(n), dma(n), dma(n),
            dma(layers * layers), dma(layers), dma(layers), dma(layers),
            dma(2 * groups * layers), dma(2 * groups * layers),
            dma(2 * groups * layers), dma(2 * groups * layers),
        ],
        compiler_params=pltpu.CompilerParams(
            collective_id=0, has_side_effects=True, vmem_limit_bytes=56 * 1024 * 1024
        ),
    )(queries, encoder_rows, key_weight, value_weight, out_weight)


def solution(mesh):
    groups, n = mesh.shape["groups"], mesh.shape["ctx"]
    return jax.shard_map(
        functools.partial(per_device, groups, n),
        mesh=mesh,
        in_specs=(P(("groups", "ctx"), None), P(("groups", "ctx"), None), P(), P(), P(None, "ctx")),
        out_specs=P(("groups", "ctx"), None),
        check_vma=False,
    )
```

```python
import functools
import math

import jax
import jax.numpy as jnp
from jax import lax
from jax.experimental import pallas as pl
from jax.experimental.pallas import tpu as pltpu
from jax.sharding import PartitionSpec as P

HEADS = 16
DH = 64
PAIR = 2 * DH
MESH = pl.DeviceIdType.MESH
LOG2E = 1.4426950408889634
ORDER = (
    "o", "n", "p0", "p1", "p2", "p3", "Q", "q0", "z1", "f", "y0", "r1",
    "q3", "q2", "q1", "y1", "z2", "r2", "K", "a0", "x1", "x0", "y2", "a1",
    "z3", "a2", "a3", "y3", "x2", "x3",
)


def kernel(
    groups, n, plane, chunks,
    q_hbm, e_hbm, kw_hbm, vw_hbm, ow_hbm, o_ref,
    q_ref, e_ref, kw, vw, qpack, kvpack, qall, kvall, keys2, vals2, cpack, call, ctx, total, wall,
    load_sem, own_sem, q_send, q_recv, kv_send, kv_recv, c_send, c_recv,
    z_send, z_recv, y_send, y_recv, x_send, x_recv, b_send, b_recv,
):
    grp = lax.axis_index("groups")
    me = lax.axis_index("ctx")
    rows = q_ref.shape[0]
    enc = e_ref.shape[0]
    depth = wall.shape[1]
    width = wall.shape[2]
    copies = n // HEADS
    share = rows // copies
    half = share // 2
    part = depth // groups
    layers = n // plane
    zed = me // plane
    spot = me % plane
    far = plane // 2
    over = zed * plane + (spot + far) % plane
    mate = zed * plane + (spot // 2) * 2 + (1 - spot % 2)
    heads = HEADS // chunks
    bf16 = jnp.bfloat16

    barrier = pltpu.get_barrier_semaphore()

    def greet(i, carry):
        pl.semaphore_signal(
            barrier, inc=1, device_id=(grp, (me + i) % n), device_id_type=MESH
        )
        return carry

    lax.fori_loop(1, n, greet, 0)
    for g in range(1, groups):
        pl.semaphore_signal(
            barrier, inc=1, device_id=((grp + g) % groups, me), device_id_type=MESH
        )

    load_q = pltpu.make_async_copy(q_hbm, q_ref, own_sem.at[0])
    load_w = pltpu.make_async_copy(ow_hbm, wall.at[me], own_sem.at[1])
    load_e = pltpu.make_async_copy(e_hbm, e_ref, own_sem.at[2])
    offsets = sorted(range(chunks), key=lambda i: (-min(i, chunks - i), i))

    def chunk_at(i):
        return (zed + offsets[i]) % chunks

    def loads(i):
        wide = kw.shape[2]
        cols = pl.ds(pl.multiple_of(chunk_at(i) * wide, wide), wide)
        return (
            pltpu.make_async_copy(kw_hbm.at[:, cols], kw.at[i], load_sem.at[i]),
            pltpu.make_async_copy(vw_hbm.at[:, cols], vw.at[i], load_sem.at[chunks + i]),
        )

    load_e.start()
    for i in range(chunks):
        for copy in loads(i):
            copy.start()
        if i == 0:
            load_q.start()
            load_w.start()

    def remote(src, dst, send, recv, to):
        return pltpu.make_async_remote_copy(
            src_ref=src, dst_ref=dst, send_sem=send, recv_sem=recv,
            device_id=to, device_id_type=MESH,
        )

    def q_copy(d, s):
        return remote(qpack.at[d], qall.at[s], q_send.at[d], q_recv.at[s], (grp, d))

    def kv_copy(d, s):
        return remote(
            kvpack.at[d % HEADS], kvall.at[pl.ds(s * enc, enc)],
            kv_send.at[d], kv_recv.at[s], (grp, d),
        )

    def c_copy(d, s):
        return remote(cpack.at[d], call.at[s], c_send.at[d], c_recv.at[s], (grp, d))

    mine = pl.ds(grp * part, part)

    def z_copy(src, to, own=False):
        block = wall.at[src * plane + spot, mine]
        return remote(
            ow_hbm.at[mine] if own else block, block, z_send.at[src * layers + to], z_recv.at[src],
            (grp, to * plane + spot),
        )

    middle = layers // 2

    def hop(act, across):
        for to in range(layers):
            if across:
                near = ((zed < middle - 1) & (to == middle)) | ((zed > middle) & (to == middle - 1))
            else:
                near = ((zed < middle) & ((to < middle) | ((to == middle) & (zed == middle - 1)))) | (
                    (zed >= middle) & ((to >= middle) | ((to == middle - 1) & (zed == middle)))
                )

            @pl.when(near & (zed != to))
            def _(to=to):
                act(z_copy(zed, to, True))

    def relay(src, act):
        for to in range(layers):
            if to > middle:

                @pl.when((zed == middle) & (src < middle))
                def _(to=to):
                    act(z_copy(src, to))

            if to < middle - 1:

                @pl.when((zed == middle - 1) & (src >= middle))
                def _(to=to):
                    act(z_copy(src, to))

    def y_copy(layer, at, to, own=False):
        block = wall.at[layer * plane + at, mine]
        return remote(ow_hbm.at[mine] if own else block, block, y_send.at[layer], y_recv.at[layer], (grp, to))

    def x_copy(layer, side, g, whose):
        at = layer * plane + (spot + side * far) % plane
        block = wall.at[at, pl.ds(whose * part, part)]
        slot = (g * 2 + side) * layers + layer
        return remote(
            block, block, x_send.at[slot], x_recv.at[slot], ((grp + g) % groups, me)
        )

    def b_copy(layer, side, g, at):
        whose = (grp + groups - g) % groups
        block = wall.at[layer * plane + (at + side * far) % plane, pl.ds(whose * part, part)]
        slot = (g * 2 + side) * layers + layer
        return remote(block, block, b_send.at[slot], b_recv.at[slot], (grp, mate))

    def whole_copy(side, at):
        block = wall.at[zed * plane + (at + side * far) % plane]
        slot = side * layers + zed
        return remote(ow_hbm, block, b_send.at[slot], b_recv.at[slot], (grp, mate))

    def some(first, last, body):
        def step(i, carry):
            body((me + i) % n)
            return carry

        lax.fori_loop(first, last, step, 0)

    def others(body):
        some(1, n, body)

    def beyond(body):
        def step(i, carry):
            body((zed + i) % layers)
            return carry

        lax.fori_loop(1, layers, step, 0)

    def far_first(body):
        def step(i, carry):
            d = (me + n // 2 + i) % n

            @pl.when(d != me)
            def _():
                body(d)

            return carry

        lax.fori_loop(0, n, step, 0)

    def sources(k, body):
        for src in (zed - k, zed + k):

            @pl.when((src >= 0) & (src < layers))
            def _(src=src):
                body(src)

    def on_z(src):
        z_copy(src, zed).wait_recv()
        y_copy(src, spot, over).start()
        for g in range(1, groups):
            x_copy(src, 0, g, grp).start()
        b_copy(src, 0, 0, spot).start()

    def on_y(src):
        y_copy(src, (spot + far) % plane, over).wait_recv()
        for g in range(1, groups):
            x_copy(src, 1, g, grp).start()
        b_copy(src, 1, 0, spot).start()

    def on_x(src):
        for g in range(1, groups):
            for side in range(2):
                x_copy(src, side, g, (grp + groups - g) % groups).wait_recv()
                b_copy(src, side, g, spot).start()

    def on_far(src):
        for g in range(1, groups):
            x_copy(src, 1, g, (grp + groups - g) % groups).wait_recv()
            b_copy(src, 1, g, spot).start()

    events = {"y0": lambda: on_y(zed), "x0": lambda: on_far(zed)}
    for k in range(1, layers):
        events[f"z{k}"] = functools.partial(sources, k, on_z)
        events[f"r{k}"] = functools.partial(sources, k, lambda src: relay(src, lambda copy: copy.start()))
        events[f"y{k}"] = functools.partial(sources, k, on_y)
        events[f"x{k}"] = functools.partial(sources, k, on_x)

    pl.semaphore_wait(barrier, n - 1 + groups - 1)
    def pack_q():
        load_q.wait()
        for d in range(n):
            r0, c0 = (d // HEADS) * share, (d % HEADS) * DH
            qpack[d] = jnp.concatenate(
                [q_ref[r0 : r0 + half, c0 : c0 + DH], q_ref[r0 + half : r0 + share, c0 : c0 + DH]],
                axis=1,
            )
        qall[me] = qpack[me]

    def start_own():
        hop(lambda copy: copy.start(), False)

    def start_across():
        hop(lambda copy: copy.start(), True)

    def start_near():
        y_copy(zed, spot, over, True).start()
        whole_copy(0, spot).start()

    def project(i):
        if i == 0:
            load_e.wait()
        one, two = loads(i)
        one.wait()
        two.wait()
        j = chunk_at(i)
        keys = jnp.dot(e_ref[...], kw[i], preferred_element_type=jnp.float32).astype(bf16)
        values = jnp.dot(e_ref[...], vw[i], preferred_element_type=jnp.float32).astype(bf16)
        for h in range(heads):
            cols = slice(h * DH, (h + 1) * DH)
            kvpack[j * heads + h] = jnp.concatenate([keys[:, cols], values[:, cols]], axis=1)

    def send_kv(i):
        j = chunk_at(i)
        for c in range(copies):
            for h in range(heads):
                d = c * HEADS + j * heads + (h + spot) % heads

                @pl.when(d != me)
                def _(d=d):
                    kv_copy(d, me).start()

    def project_and_send(i):
        project(i)
        send_kv(i)

    def apart(k):
        at, bit = me, 1
        while bit <= k:
            if k & bit:
                at = at + bit * (1 - 2 * (me // bit % 2))
            bit *= 2
        return at

    def send_q(first, last):
        for k in range(last - 1, first - 1, -1):
            if k:
                q_copy(apart(k), me).start()

    def take_kv():
        kvall[pl.ds(me * enc, enc)] = kvpack[me % HEADS]
        others(lambda s: kv_copy(s, s).wait_recv())
        memory = kvall[...]
        nothing, ones = jnp.zeros((n * enc, DH), bf16), jnp.ones((n * enc, DH), bf16)
        keys2[0] = jnp.concatenate([memory[:, :DH], nothing], axis=1)
        keys2[1] = jnp.concatenate([nothing, memory[:, :DH]], axis=1)
        vals2[0] = jnp.concatenate([memory[:, DH:], ones], axis=1)
        vals2[1] = jnp.concatenate([ones, memory[:, DH:]], axis=1)

    together = min(n, max(1, 256 // half))
    left = lax.broadcasted_iota(jnp.int32, (together * half, PAIR), 1) < DH

    steps = n // together

    def attend(i):
        whose = [apart(k) for k in range(i * together, (i + 1) * together)]
        for k, s in zip(range(i * together, (i + 1) * together), whose):
            if k:
                q_copy(s, s).wait_recv()

        query = jnp.concatenate([qall[s] for s in whose], axis=0)
        summed = []
        for side in range(2):
            scores = lax.dot_general(
                query, keys2[side], (((1,), (1,)), ((), ())), preferred_element_type=jnp.float32
            )
            top = jnp.max(scores, axis=1, keepdims=True)
            expo = jnp.exp2((scores - top) * (0.125 * LOG2E)).astype(bf16)
            summed.append(jnp.dot(expo, vals2[side], preferred_element_type=jnp.float32))
        over_total = jnp.where(left, summed[1], summed[0])
        out = (jnp.where(left, summed[0], summed[1]) / pltpu.roll(over_total, DH, 1)).astype(bf16)
        for j, s in enumerate(whose):
            cpack[s] = out[j * half : (j + 1) * half]
        return whose

    def send(whose):
        for s in whose:

            @pl.when(s != me)
            def _(s=s):
                c_copy(s, me).start()


    def turn(i):
        send(attend(i))

    steps = n // together
    acts = dict(events)
    acts["Q"] = pack_q
    acts["o"], acts["n"], acts["K"], acts["f"] = start_own, start_near, take_kv, start_across
    for i in range(chunks):
        acts[f"p{i}"] = functools.partial(project_and_send, i)
        acts[f"c{i}"] = functools.partial(project, i)
        acts[f"s{i}"] = functools.partial(send_kv, i)
    for i in range(4):
        acts[f"q{i}"] = functools.partial(send_q, n * i // 4, n * (i + 1) // 4)
    for i in range(steps):
        acts[f"a{i}"] = functools.partial(turn, i)
    rest = [f"a{i}" for i in range(steps)]
    for k in range(1, layers):
        rest += [f"z{k}", f"r{k}", f"y{k}", f"x{k}"]
    known = [name for name in ORDER if name in acts]
    for name in known + [name for name in rest if name not in known]:
        acts[name]()

    load_w.wait()
    call[me] = cpack[me]
    mates = mate % plane

    def take_b(z):
        for g in range(groups):
            for side in range(2):
                b_copy(z, side, g, mates).wait_recv()

    def take_rest():
        whole_copy(0, mates).wait_recv()
        for g in range(groups):
            b_copy(zed, 1, g, mates).wait_recv()
        beyond(take_b)

    near = n // 2
    base = me // near * near

    def unpack(at):
        for j in range(0, near, 2):
            one, two = call[at + j], call[at + j + 1]
            cols = pl.ds(pl.multiple_of((at + j) * DH, PAIR), PAIR)
            ctx[:half, cols] = jnp.concatenate([one[:, :DH], two[:, :DH]], axis=1)
            ctx[half:, cols] = jnp.concatenate([one[:, DH:], two[:, DH:]], axis=1)

    def product(at, d):
        heads_at = pl.ds(pl.multiple_of(at * DH, near * DH), near * DH)
        pair = jnp.concatenate([wall[d, heads_at], wall[d + 1, heads_at]], axis=1)
        return jnp.dot(ctx[:, heads_at], pair, preferred_element_type=jnp.float32)

    if copies == 1:
        for k in range(1, near):
            c_copy(apart(k), apart(k)).wait_recv()
        unpack(base)
        take_rest()
        for d in range(0, n, 2):
            total[:, d * width : (d + 2) * width] = product(base, d)
        for k in range(near, n):
            c_copy(apart(k), apart(k)).wait_recv()
        unpack(near - base)
        for d in range(0, n, 2):
            cols = slice(d * width, (d + 2) * width)
            o_ref[:, cols] = (total[:, cols] + product(near - base, d)).astype(bf16)
    else:
        take_rest()
        others(lambda s: c_copy(s, s).wait_recv())
        for c in range(copies):
            for j in range(HEADS // 2):
                one, two = call[c * HEADS + 2 * j], call[c * HEADS + 2 * j + 1]
                r0, cols = c * share, slice(j * PAIR, (j + 1) * PAIR)
                ctx[r0 : r0 + half, cols] = jnp.concatenate([one[:, :DH], two[:, :DH]], axis=1)
                ctx[r0 + half : r0 + share, cols] = jnp.concatenate([one[:, DH:], two[:, DH:]], axis=1)
        for d in range(0, n, 2):
            pair = jnp.concatenate([wall[d], wall[d + 1]], axis=1)
            o_ref[:, d * width : (d + 2) * width] = jnp.dot(
                ctx[...], pair, preferred_element_type=jnp.float32
            ).astype(bf16)

    def sent(d):
        q_copy(d, me).wait_send()
        kv_copy(d, me).wait_send()
        c_copy(d, me).wait_send()

    others(sent)

    def sent_layer(z):
        relay(z, lambda copy: copy.wait_send())
        y_copy(z, spot, over).wait_send()
        for side in range(2):
            for g in range(1, groups):
                x_copy(z, side, g, grp).wait_send()
            for g in range(groups):
                b_copy(z, side, g, spot).wait_send()

    beyond(sent_layer)
    hop(lambda copy: copy.wait_send(), False)
    hop(lambda copy: copy.wait_send(), True)
    y_copy(zed, spot, over, True).wait_send()
    for g in range(1, groups):
        x_copy(zed, 1, g, grp).wait_send()
        b_copy(zed, 1, g, spot).wait_send()
    b_copy(zed, 1, 0, spot).wait_send()
    whole_copy(0, spot).wait_send()


def per_device(groups, n, queries, encoder_rows, key_weight, value_weight, out_weight):
    rows, wide = queries.shape
    enc, model = encoder_rows.shape
    depth, width = out_weight.shape
    plane = math.gcd(n, 4)
    layers = n // plane
    chunks = 4
    half = rows // (n // HEADS) // 2
    bf16 = jnp.bfloat16
    dma = lambda k: pltpu.SemaphoreType.DMA((k,))
    hbm = pl.BlockSpec(memory_space=pl.ANY)
    return pl.pallas_call(
        functools.partial(kernel, groups, n, plane, chunks),
        out_shape=pltpu.VMEM((rows, n * width), bf16),
        in_specs=[hbm] * 5,
        out_specs=pl.BlockSpec(memory_space=pltpu.VMEM),
        scratch_shapes=[
            pltpu.VMEM((rows, wide), bf16),
            pltpu.VMEM((enc, model), bf16),
            pltpu.VMEM((chunks, model, wide // chunks), bf16),
            pltpu.VMEM((chunks, model, wide // chunks), bf16),
            pltpu.VMEM((n, half, PAIR), bf16),
            pltpu.VMEM((HEADS, enc, PAIR), bf16),
            pltpu.VMEM((n, half, PAIR), bf16),
            pltpu.VMEM((n * enc, PAIR), bf16),
            pltpu.VMEM((2, n * enc, PAIR), bf16),
            pltpu.VMEM((2, n * enc, PAIR), bf16),
            pltpu.VMEM((n, half, PAIR), bf16),
            pltpu.VMEM((n, half, PAIR), bf16),
            pltpu.VMEM((rows, depth), bf16),
            pltpu.VMEM((rows, n * width), jnp.float32),
            pltpu.VMEM((n, depth, width), bf16),
            dma(2 * chunks),
            dma(3),
            dma(n), dma(n), dma(n), dma(n), dma(n), dma(n),
            dma(layers * layers), dma(layers), dma(layers), dma(layers),
            dma(2 * groups * layers), dma(2 * groups * layers),
            dma(2 * groups * layers), dma(2 * groups * layers),
        ],
        compiler_params=pltpu.CompilerParams(
            collective_id=0, has_side_effects=True, vmem_limit_bytes=56 * 1024 * 1024
        ),
    )(queries, encoder_rows, key_weight, value_weight, out_weight)


def solution(mesh):
    groups, n = mesh.shape["groups"], mesh.shape["ctx"]
    return jax.shard_map(
        functools.partial(per_device, groups, n),
        mesh=mesh,
        in_specs=(P(("groups", "ctx"), None), P(("groups", "ctx"), None), P(), P(), P(None, "ctx")),
        out_specs=P(("groups", "ctx"), None),
        check_vma=False,
    )
```
